32 devices in a mesh: seq: 4 (over z), fsdp: 8 (over y, x, core).
Axes of the slice: x: 2, y: 2, z: 4, core: 2. Of those that a mesh axis runs over, the one named last changes fastest.
Arguments:
- tokens: bfloat16 [8, 1024, 2048], P('fsdp', 'seq'), may hold values from -6 to 6
- attention_gain: bfloat16 [2048], P('fsdp'), may hold values from 0.099609375 to 1.8984375
- query_weight: bfloat16 [2048, 2048], P('fsdp'), may hold values from -0.125 to 0.125
- key_projection_weight: bfloat16 [2048, 1024], P('fsdp'), may hold values from -0.125 to 0.125
- value_projection_weight: bfloat16 [2048, 1024], P('fsdp'), may hold values from -0.125 to 0.125
- query_gain: bfloat16 [128], P('fsdp'), may hold values from 0.099609375 to 1.8984375
- key_gain: bfloat16 [128], P('fsdp'), may hold values from 0.099609375 to 1.8984375
- output_weight: bfloat16 [2048, 2048], P('fsdp'), may hold values from -2 to 2
- feed_gain: bfloat16 [2048], P('fsdp'), may hold values from 0.099609375 to 1.8984375
- gate_weight: bfloat16 [2048, 6144], P('fsdp'), may hold values from -0.125 to 0.125
- up_weight: bfloat16 [2048, 6144], P('fsdp'), may hold values from -0.125 to 0.125
- down_weight: bfloat16 [6144, 2048], P('fsdp'), may hold values from -0.078125 to 0.078125
- cotangent: bfloat16 [8, 1024, 2048], P('fsdp', 'seq'), may hold values from -6 to 6
- seq_lengths: int32 [24], replicated, may hold values from 256 to 512, as said below
- dealing: int32 [24], replicated, may hold values from 0 to 23, as said below
Outputs:
- mixed: bfloat16 [8, 1024, 2048], P('fsdp', 'seq')
- input_gradient: bfloat16 [8, 1024, 2048], P('fsdp', 'seq')
- attention_gain_gradient: float32 [2048], P('fsdp')
- query_weight_gradient: float32 [2048, 2048], P('fsdp')
- key_weight_gradient: float32 [2048, 1024], P('fsdp')
- value_weight_gradient: float32 [2048, 1024], P('fsdp')
- query_gain_gradient: float32 [128], P('fsdp')
- key_gain_gradient: float32 [128], P('fsdp')
- output_weight_gradient: float32 [2048, 2048], P('fsdp')
- feed_gain_gradient: float32 [2048], P('fsdp')
- gate_weight_gradient: float32 [2048, 6144], P('fsdp')
- up_weight_gradient: float32 [2048, 6144], P('fsdp')
- down_projection_gradient: float32 [6144, 2048], P('fsdp')
The draws below stay inside these ranges and needn't reach their ends.
Inputs may be any that keep to these rules, and one draw needn't show every extreme that they name: `seq_lengths`: the sequences dealt to one group sum to at most 1024 tokens; in some group one sequence is 512 long and the group has no padding. A permutation of the 24 sequences; group g packs dealing[g * 3] to dealing[g * 3 + 2].
All inputs are finite; a program needn't handle non-finite values.
Results may differ from the reference program's by a relative error of at most 0.02.
Values may be sent and summed in bfloat16 or wider, within the bound.
No kernel may reach another device: no remote copies, remote signals or barrier semaphores. Data moves between devices by JAX's collectives and lax.ppermute only.
A program may use at most 512 MiB of HBM per device.

```python
import jax
import jax.numpy as jnp
from jax import lax

MODEL_WIDTH = 2048
HQ = 16
KEY_VALUE_HEADS = 8
HEAD_WIDTH = 128
FF = 6144
SLOTS = 3
MIN_LEN = 256
GROUP = 1024
GROUPS = 8


def dealt_table(key):
    group_span = GROUP
    group_count = GROUPS
    first_key, second_key, third_key, fourth_key = jax.random.split(jax.random.fold_in(key, 4242), 4)
    spare_room = group_span - SLOTS * MIN_LEN
    padding = jax.random.randint(first_key, (group_count,), 0, group_span // 4 + 1)
    full_group = jax.random.randint(fourth_key, (), 0, group_count)
    group_ids = jnp.arange(group_count, dtype=jnp.int32)
    padding = jnp.where(group_ids == full_group, 0, padding)
    free_room = (spare_room - padding).astype(jnp.int32)
    cut_points = jax.random.randint(second_key, (group_count, SLOTS - 1), 0, free_room[:, None] + 1)
    cut_points = jnp.sort(cut_points, axis=1)
    cut_edges = jnp.concatenate([jnp.zeros((group_count, 1), jnp.int32), cut_points, free_room[:, None]], axis=1)
    extra_length = cut_edges[:, 1:] - cut_edges[:, :-1]
    longest_row = jnp.zeros((SLOTS,), jnp.int32).at[0].set(spare_room)
    extra_length = jnp.where((group_ids == full_group)[:, None], longest_row[None, :], extra_length)
    length_table = (MIN_LEN + extra_length).astype(jnp.int32)
    dealt_order = jax.random.permutation(third_key, group_count * SLOTS).astype(jnp.int32)
    lengths = jnp.zeros((group_count * SLOTS,), jnp.int32).at[dealt_order].set(length_table.reshape(-1))
    return (lengths, dealt_order)


def draw_seq_lengths(key, part):
    return dealt_table(key)[0]


def draw_dealing(key, part):
    return dealt_table(key)[1]


def levels(rng, dims, shards, low, high):
    level = 1.0
    for dim, shards_of in shards:
        draws = jax.random.uniform(jax.random.fold_in(jax.random.fold_in(rng, 6), dim), (shards_of,), jnp.float32, low / len(shards), high / len(shards))
        level = level * jnp.repeat(jnp.exp(draws), dims[dim] // shards_of).reshape((-1,) + (1,) * (len(dims) - 1 - dim))
    return level


def noise(key, dims, width, bound, cuts=(), kind=jnp.bfloat16):
    result = jax.random.normal(key, dims, jnp.float32) * width
    if len(cuts) > 0:
        result = levels(key, dims, cuts, -0.22, 0.18) * result
    return jnp.clip(result, min=-bound, max=bound).astype(kind)


def setup_inputs(seed: int = 0) -> dict:
    splits = jax.random.split(jax.random.key(seed), 16)
    tokens = noise(splits[0], (GROUPS, GROUP, MODEL_WIDTH), 1.0, 6.0, ((0, 8), (1, 4)))
    attention_gain = jnp.clip(1.0 + 0.18 * jax.random.normal(splits[1], (MODEL_WIDTH,), jnp.float32), 0.099609375, 1.8984375).astype(jnp.bfloat16)
    query_weight = noise(splits[2], (MODEL_WIDTH, HQ * HEAD_WIDTH), MODEL_WIDTH ** -0.5, 0.125, ((0, 8),))
    key_projection_weight = noise(splits[3], (MODEL_WIDTH, KEY_VALUE_HEADS * HEAD_WIDTH), MODEL_WIDTH ** -0.5, 0.125, ((0, 8),))
    value_projection_weight = noise(splits[4], (MODEL_WIDTH, KEY_VALUE_HEADS * HEAD_WIDTH), MODEL_WIDTH ** -0.5, 0.125, ((0, 8),))
    query_gain = jnp.clip(1.0 + 0.18 * jax.random.normal(splits[5], (HEAD_WIDTH,), jnp.float32), 0.099609375, 1.8984375).astype(jnp.bfloat16)
    key_gain = jnp.clip(1.0 + 0.18 * jax.random.normal(splits[6], (HEAD_WIDTH,), jnp.float32), 0.099609375, 1.8984375).astype(jnp.bfloat16)
    output_weight = noise(splits[7], (HQ * HEAD_WIDTH, MODEL_WIDTH), (max(HQ * HEAD_WIDTH * 4 // GROUP, 1)) ** -0.5, 2.0, ((0, 8),))
    feed_gain = jnp.clip(1.0 + 0.18 * jax.random.normal(splits[8], (MODEL_WIDTH,), jnp.float32), 0.099609375, 1.8984375).astype(jnp.bfloat16)
    gate_weight = noise(splits[9], (MODEL_WIDTH, FF), MODEL_WIDTH ** -0.5, 0.125, ((0, 8),))
    up_weight = noise(splits[10], (MODEL_WIDTH, FF), MODEL_WIDTH ** -0.5, 0.125, ((0, 8),))
    down_weight = noise(splits[11], (FF, MODEL_WIDTH), FF ** -0.5, 0.078125, ((0, 8),))
    cotangent = noise(splits[12], (GROUPS, GROUP, MODEL_WIDTH), 1.0, 6.0, ((0, 8), (1, 4)))
    seq_lengths = draw_seq_lengths(jax.random.fold_in(splits[15], 71), 0)
    dealing = draw_dealing(jax.random.fold_in(splits[15], 71), 0)
    return {"tokens": tokens, "attention_gain": attention_gain, "query_weight": query_weight, "key_projection_weight": key_projection_weight, "value_projection_weight": value_projection_weight, "query_gain": query_gain, "key_gain": key_gain, "output_weight": output_weight, "feed_gain": feed_gain, "gate_weight": gate_weight, "up_weight": up_weight, "down_weight": down_weight, "cotangent": cotangent, "seq_lengths": seq_lengths, "dealing": dealing}


EPSILON = 1e-06
ROPE_BASE = 1000000.0
NEGATIVE = -1e+30
HIGHEST = lax.Precision.HIGHEST

@jax.custom_vjp
def low(v):
    return lax.optimization_barrier(v.astype(jnp.bfloat16)).astype(jnp.float32)

@jax.custom_vjp
def low_back(v):
    return v

def low_keep(v):
    return (low(v), None)

def low_pass(kept, grad):
    return (grad,)

def back_keep(v):
    return (v, None)

def back_low(kept, grad):
    return (low(grad),)
low.defvjp(low_keep, low_pass)
low_back.defvjp(back_keep, back_low)

def group_layout(seq_lengths, dealing, group_index, group_span, slot_count):
    dealt_ids = lax.dynamic_slice_in_dim(dealing, group_index * slot_count, slot_count)
    seq_numbers = jnp.arange(seq_lengths.shape[0], dtype=jnp.int32)
    dealt_lengths = lax.optimization_barrier(jnp.sum(jnp.where(dealt_ids[:, None] == seq_numbers[None, :], seq_lengths[None, :], 0), axis=1)).astype(jnp.int32)
    seq_ends = jnp.cumsum(dealt_lengths).astype(jnp.int32)
    seq_starts = jnp.concatenate([jnp.zeros((1,), jnp.int32), seq_ends]).astype(jnp.int32)
    row_index = jnp.arange(group_span, dtype=jnp.int32)
    segment = lax.optimization_barrier(jnp.sum((row_index[:, None] >= seq_ends[None, :]).astype(jnp.int32), axis=1)).astype(jnp.int32)
    slot_marks = jnp.arange(slot_count + 1, dtype=jnp.int32)
    seq_begin = lax.optimization_barrier(jnp.sum(jnp.where(segment[:, None] == slot_marks[None, :], seq_starts[None, :], 0), axis=1)).astype(jnp.int32)
    return (segment, row_index - seq_begin)

def turned(values, position, direction):
    half_size = values.shape[-1] // 2
    exponent = jnp.arange(half_size, dtype=jnp.float32) * (2.0 / values.shape[-1])
    frequency = ROPE_BASE ** (-exponent)
    angles = position.astype(jnp.float32)[:, None] * frequency[None, :]
    cosine = jnp.cos(angles)[:, None, :]
    sine = jnp.sin(angles)[:, None, :]
    lower_half = values[..., :half_size]
    upper_half = values[..., half_size:]
    return jnp.concatenate([lower_half * cosine - direction * upper_half * sine, upper_half * cosine + direction * lower_half * sine], axis=-1)

def rms_norm(values, gain):
    return values * lax.rsqrt(lax.optimization_barrier(jnp.mean(values * values, axis=-1, keepdims=True)) + EPSILON) * gain

def product(left, right):
    return jnp.dot(left, right, precision=HIGHEST)

def attend(queries, keys, values, segment):
    group_span, head_count, head_size = queries.shape
    repeat_count = head_count // keys.shape[1]
    keys_wide = jnp.repeat(keys, repeat_count, axis=1)
    values_wide = jnp.repeat(values, repeat_count, axis=1)
    block_rows = min(512, group_span)
    row_index = jnp.arange(group_span, dtype=jnp.int32)
    score_scale = head_size ** (-0.5)

    def one_block(first_row):
        query_block = lax.dynamic_slice_in_dim(queries, first_row, block_rows, 0)
        segment_block = lax.dynamic_slice_in_dim(segment, first_row, block_rows, 0)
        index_block = lax.dynamic_slice_in_dim(row_index, first_row, block_rows, 0)
        scores = low_back(jnp.einsum('qhd,khd->hqk', query_block, keys_wide, precision=HIGHEST) * score_scale)
        allowed = (segment_block[:, None] == segment[None, :]) & (index_block[:, None] >= row_index[None, :])
        scores = jnp.where(allowed[None], scores, NEGATIVE)
        probabilities = jax.nn.softmax(scores, axis=-1)
        return jnp.einsum('hqk,khd->qhd', low(probabilities), values_wide, precision=HIGHEST)
    first_rows = jnp.arange(group_span // block_rows, dtype=jnp.int32) * block_rows
    blocks = lax.map(jax.checkpoint(one_block), first_rows)
    return blocks.reshape(group_span, head_count, head_size)

def one_group(inputs, params, segment, position):
    gain_one, query_matrix, key_matrix, value_matrix, query_norm, key_norm, output_matrix, gain_two, gate_matrix, up_matrix, down_matrix = params
    head_size = query_norm.shape[0]
    query_heads = query_matrix.shape[1] // head_size
    key_heads = key_matrix.shape[1] // head_size
    group_span = inputs.shape[0]
    normed_one = low(rms_norm(inputs, gain_one))
    query_proj = low_back(product(normed_one, query_matrix)).reshape(group_span, query_heads, head_size)
    key_proj = low_back(product(normed_one, key_matrix)).reshape(group_span, key_heads, head_size)
    value_rows = low(low_back(product(normed_one, value_matrix))).reshape(group_span, key_heads, head_size)
    query_rows = low(low_back(turned(rms_norm(query_proj, query_norm), position, 1.0)))
    key_rows = low(low_back(turned(rms_norm(key_proj, key_norm), position, 1.0)))
    attended = low(low_back(attend(query_rows, key_rows, value_rows, segment))).reshape(group_span, query_heads * head_size)
    residual = inputs + low_back(product(attended, output_matrix))
    normed_two = low(rms_norm(residual, gain_two))
    gate_value = low_back(product(normed_two, gate_matrix))
    up_value = low_back(product(normed_two, up_matrix))
    hidden = low(jax.nn.silu(gate_value) * up_value)
    return residual + low_back(product(hidden, down_matrix))

def reference(tokens, attention_gain, query_weight, key_projection_weight, value_projection_weight, query_gain, key_gain, output_weight, feed_gain, gate_weight, up_weight, down_weight, cotangent, seq_lengths, dealing):
    group_count = tokens.shape[0]
    group_span = tokens.shape[1]
    slot_count = dealing.shape[0] // group_count
    group_ids = jnp.arange(group_count, dtype=jnp.int32)
    segments, positions = jax.vmap(lambda index: group_layout(seq_lengths, dealing, index, group_span, slot_count))(group_ids)
    params = tuple((weight.astype(jnp.float32) for weight in (attention_gain, query_weight, key_projection_weight, value_projection_weight, query_gain, key_gain, output_weight, feed_gain, gate_weight, up_weight, down_weight)))
    inputs = tokens.astype(jnp.float32)

    def forward(inputs_all, weights):

        def step(unused, pieces):
            group_tokens, segment, position = pieces
            return (unused, jax.checkpoint(one_group)(group_tokens, weights, segment, position))
        return lax.scan(step, jnp.zeros((), jnp.float32), (inputs_all, segments, positions))[1]
    mixed, pullback = jax.vjp(forward, inputs, params)
    input_gradient, weight_gradients = pullback(cotangent.astype(jnp.float32))
    return (mixed.astype(jnp.bfloat16), input_gradient.astype(jnp.bfloat16)) + tuple(weight_gradients)
```

```python
import jax
import jax.numpy as jnp
from jax import lax
from jax.sharding import PartitionSpec as P

EPSILON = 1e-06
ROPE_BASE = 1000000.0
NEGATIVE = -1e30
F32 = jnp.float32
BF16 = jnp.bfloat16


def relocation(ns, nf):
    pairs = []
    for s in range(ns):
        for g in range(nf):
            p, c = divmod(g, 2)
            pairs.append((s * nf + g, p * nf + 2 * (p ^ s ^ (ns // 2 * c)) + c))
    return pairs


def move(values, pairs):
    return lax.ppermute(values, ("seq", "fsdp"), pairs)


def swap(values, k):
    n = lax.axis_size("fsdp")
    return lax.ppermute(values, "fsdp", [(i, i ^ k) for i in range(n)])


def exchange(piece_for, step=1):
    n, me = lax.axis_size("fsdp"), lax.axis_index("fsdp")
    got = {0: piece_for(me)}
    for k in range(step, n, step):
        got[k] = swap(piece_for(me ^ k), k)
    return got


def assembled(got, step=1):
    n, me = lax.axis_size("fsdp"), lax.axis_index("fsdp")
    buffer = jnp.zeros((n // step,) + got[0].shape, got[0].dtype)
    for k, piece in got.items():
        buffer = lax.dynamic_update_index_in_dim(buffer, piece, (me ^ k) // step, 0)
    return buffer


def pick(blocks, index):
    return lax.dynamic_index_in_dim(blocks, index, 0, keepdims=False)


def line_sums(chunks):
    ns = lax.axis_size("seq")
    if ns != 4:
        return [lax.psum(c, "seq") for c in chunks]
    me = lax.axis_index("seq")
    outer = (me == 0) | (me == 3)
    count = len(chunks)
    first, second, totals, sums = {}, {}, {}, [None] * count
    arrived, crossed = {}, {}
    token = None
    for step in range(count + 2):
        sends = []
        if step < count:
            sends.append(("a", step, chunks[step], [(0, 1), (3, 2)]))
        if 0 <= step - 1 < count:
            i = step - 1
            first[i] = (chunks[i].astype(F32) + arrived[i].astype(F32)).astype(BF16)
            sends.append(("b", i, first[i], [(1, 2), (2, 1)]))
        if 0 <= step - 2 < count:
            i = step - 2
            totals[i] = (first[i].astype(F32) + crossed[i].astype(F32)).astype(BF16)
            sends.append(("c", i, totals[i], [(1, 0), (2, 3)]))
        operands = [s[2] for s in sends]
        if token is not None:
            operands, _ = lax.optimization_barrier((operands, token))
        results = [lax.ppermute(o, "seq", s[3]) for o, s in zip(operands, sends)]
        token = [r[:1, :128] for r in results]
        for (kind, i, _, _), r in zip(sends, results):
            if kind == "a":
                arrived[i] = r
            elif kind == "b":
                crossed[i] = r
            else:
                sums[i] = jnp.where(outer, r, totals[i])
    return sums


def rope_tables(position, head):
    half = head // 2
    exponent = jnp.arange(half, dtype=F32) * (2.0 / head)
    frequency = ROPE_BASE ** (-exponent)
    angles = position.astype(F32)[:, None] * frequency[None, :]
    return jnp.cos(angles)[:, None, :], jnp.sin(angles)[:, None, :]


def turned(values, tables, direction):
    cosine, sine = tables
    half = values.shape[-1] // 2
    low, high = values[..., :half], values[..., half:]
    return jnp.concatenate(
        [low * cosine - direction * high * sine, high * cosine + direction * low * sine], axis=-1
    )


def norm_back(gradient, unit_rows, inverse):
    return inverse * (gradient - unit_rows * jnp.mean(gradient * unit_rows, axis=-1, keepdims=True))


def inverse_rms(values):
    return lax.rsqrt(jnp.mean(values * values, axis=-1, keepdims=True) + EPSILON)


def dot(left, right):
    return jnp.dot(left, right, preferred_element_type=F32)


def dot_nt(left, right):
    return jnp.einsum("ab,cb->ac", left, right, preferred_element_type=F32)


def dot_tn(left, right):
    return jnp.einsum("ta,tb->ab", left, right, preferred_element_type=F32)


def masked_scores(query, key, segment, index, scale):
    scores = jnp.einsum("grqd,gkd->grqk", query, key, preferred_element_type=F32) * scale
    allowed = (segment[:, :, None] == segment[:, None, :]) & (index[:, :, None] >= index[:, None, :])
    return jnp.where(allowed[:, None], scores, NEGATIVE)


def attend_forward(query, key, value, segment, index, scale):
    scores = masked_scores(query, key, segment, index, scale)
    row_max = jnp.max(scores, axis=-1, keepdims=True)
    weights = jnp.exp(scores - row_max)
    row_total = jnp.sum(weights, axis=-1, keepdims=True)
    probs = (weights / row_total).astype(BF16)
    result = jnp.einsum("grqk,gkd->grqd", probs, value, preferred_element_type=F32)
    return result.astype(BF16), row_max + jnp.log(row_total)


def attend_backward(query, key, value, grad, log_total, segment, index, scale):
    scores = masked_scores(query, key, segment, index, scale)
    probs = jnp.exp(scores - log_total)
    prob_grad = jnp.einsum("grqd,gkd->grqk", grad, value, preferred_element_type=F32)
    delta = jnp.sum(probs * prob_grad, axis=-1, keepdims=True)
    score_grad = (probs * (prob_grad - delta)).astype(BF16)
    query_grad = jnp.einsum("grqk,gkd->grqd", score_grad, key, preferred_element_type=F32) * scale
    key_grad = jnp.einsum("grqk,grqd->gkd", score_grad, query, preferred_element_type=F32) * scale
    value_grad = jnp.einsum(
        "grqk,grqd->gkd", probs.astype(BF16), grad, preferred_element_type=F32
    )
    return query_grad.astype(BF16), key_grad.astype(BF16), value_grad.astype(BF16)


def body(
    tokens,
    attention_gain,
    query_weight,
    key_projection_weight,
    value_projection_weight,
    query_gain,
    key_gain,
    output_weight,
    feed_gain,
    gate_weight,
    up_weight,
    down_weight,
    cotangent,
    seq_lengths,
    dealing,
):
    ns, nf = lax.axis_size("seq"), lax.axis_size("fsdp")
    plane, me = lax.axis_index("seq"), lax.axis_index("fsdp")
    rows, width = tokens.shape[1], tokens.shape[2]
    slots = dealing.shape[0] // nf
    head = query_gain.shape[0] * nf
    key_heads = key_projection_weight.shape[1] // head
    repeat = query_weight.shape[1] // head // key_heads
    share = nf // key_heads
    assert nf == 2 * ns and share in (1, 2) and key_heads * share == nf
    held = nf // share
    groups = 2 // share
    wide = repeat * head
    weight_rows = query_weight.shape[0]
    hidden_cols = gate_weight.shape[1] // nf
    scale = head ** (-0.5)
    pairs = relocation(ns, nf)
    back_pairs = [(b, a) for a, b in pairs]

    block_ids = jnp.arange(nf, dtype=jnp.int32)
    quarter = (block_ids // 2) ^ plane ^ (ns // 2 * (block_ids % 2))
    row_index = quarter[:, None] * rows + jnp.arange(rows, dtype=jnp.int32)[None, :]
    dealt = lax.dynamic_slice_in_dim(dealing, plane * 2 * slots, 2 * slots)
    numbers = jnp.arange(seq_lengths.shape[0], dtype=jnp.int32)
    lengths = jnp.sum(jnp.where(dealt[:, None] == numbers[None, :], seq_lengths[None, :], 0), axis=1)
    ends = jnp.cumsum(lengths.reshape(2, slots), axis=1)
    block_ends = jnp.where((block_ids % 2 == 0)[:, None], ends[0][None, :], ends[1][None, :])
    passed = row_index[:, :, None] >= block_ends[:, None, :]
    segment = jnp.sum(passed.astype(jnp.int32), axis=2)
    begin = jnp.max(jnp.where(passed, block_ends[:, None, :], 0), axis=2)
    position = row_index - begin

    def own(blocks):
        if share == 1:
            return blocks
        return pick(jnp.moveaxis(blocks.reshape((held, share) + blocks.shape[1:]), 1, 0), me % share)

    def by_group(values):
        heads = values.shape[1]
        split = values.reshape(held // groups, groups, rows, heads, -1)
        return split.transpose(1, 3, 0, 2, 4).reshape(groups, heads, -1, split.shape[-1])

    def from_group(values):
        heads = values.shape[1]
        split = values.reshape(groups, heads, held // groups, rows, -1)
        return split.transpose(2, 0, 3, 1, 4).reshape(held * rows, heads, -1)

    inputs = move(tokens[0], pairs).astype(F32)
    own_gradient = move(cotangent[0], pairs)

    small = jnp.concatenate([attention_gain, feed_gain, query_gain, key_gain])
    small = lax.all_gather(small, "fsdp", axis=0).astype(F32)
    cuts = [weight_rows, 2 * weight_rows, 2 * weight_rows + head // nf]
    gain_one, gain_two, query_norm, key_norm = (
        part.reshape(-1) for part in jnp.split(small, cuts, axis=1)
    )

    qkv_local = jnp.concatenate(
        [
            query_weight.reshape(weight_rows, key_heads, wide),
            key_projection_weight.reshape(weight_rows, key_heads, head),
            value_projection_weight.reshape(weight_rows, key_heads, head),
        ],
        axis=2,
    ).transpose(1, 0, 2)
    qkv_matrix = assembled(exchange(lambda d: pick(qkv_local, d // share))).reshape(
        width, wide + 2 * head
    )

    inverse_one = inverse_rms(inputs)
    unit_one = inputs * inverse_one
    normed_one = lax.all_gather(
        (unit_one * gain_one).astype(BF16), "fsdp", axis=0
    )
    normed_mine = own(normed_one).reshape(held * rows, width)
    mine_segment = own(segment)
    mine_index = own(row_index)
    tables = rope_tables(own(position).reshape(-1), head)

    projected = dot(normed_mine, qkv_matrix)
    query_proj = projected[:, :wide].reshape(-1, repeat, head)
    key_proj = projected[:, wide : wide + head].reshape(-1, 1, head)
    value_rows = projected[:, wide + head :].astype(BF16).reshape(-1, 1, head)
    query_inverse = inverse_rms(query_proj)
    query_unit = query_proj * query_inverse
    query_rows = turned(query_unit * query_norm, tables, 1.0).astype(BF16)
    key_inverse = inverse_rms(key_proj)
    key_unit = key_proj * key_inverse
    key_rows = turned(key_unit * key_norm, tables, 1.0).astype(BF16)

    group_segment = by_group(mine_segment.reshape(-1, 1, 1))[:, 0, :, 0]
    group_index = by_group(mine_index.reshape(-1, 1, 1))[:, 0, :, 0]
    group_query = by_group(query_rows)
    group_key = by_group(key_rows)[:, 0]
    group_value = by_group(value_rows)[:, 0]
    head_result, log_total = attend_forward(
        group_query, group_key, group_value, group_segment, group_index, scale
    )
    head_blocks = from_group(head_result).reshape(held, rows, wide)
    attended = assembled(exchange(lambda d: pick(head_blocks, d // share), share), share)
    attended = attended.transpose(1, 0, 2).reshape(rows, width)

    output_matrix = lax.all_gather(output_weight, "fsdp", axis=0, tiled=True)
    residual = inputs + dot(attended, output_matrix)

    gate_blocks = gate_weight.reshape(weight_rows, nf, hidden_cols).transpose(1, 0, 2)
    up_blocks = up_weight.reshape(weight_rows, nf, hidden_cols).transpose(1, 0, 2)
    gate_matrix = assembled(exchange(lambda d: pick(gate_blocks, d))).reshape(width, hidden_cols)
    up_matrix = assembled(exchange(lambda d: pick(up_blocks, d))).reshape(width, hidden_cols)
    out_gradient = lax.all_gather(own_gradient, "fsdp", axis=0, tiled=True)
    hidden_grad = dot_nt(out_gradient, down_weight)

    inverse_two = inverse_rms(residual)
    unit_two = residual * inverse_two
    normed_two = lax.all_gather((unit_two * gain_two).astype(BF16), "fsdp", axis=0, tiled=True)
    gate_value = dot(normed_two, gate_matrix)
    up_value = dot(normed_two, up_matrix)
    sigmoid_gate = jax.nn.sigmoid(gate_value)
    hidden = (gate_value * sigmoid_gate * up_value).astype(BF16)
    up_grad = (hidden_grad * gate_value * sigmoid_gate).astype(BF16)
    gate_grad = (
        hidden_grad * up_value * sigmoid_gate * (1.0 + gate_value * (1.0 - sigmoid_gate))
    ).astype(BF16)
    normed_two_part = dot_nt(gate_grad, gate_matrix) + dot_nt(up_grad, up_matrix)
    normed_two_grad = lax.psum_scatter(
        normed_two_part.astype(BF16), "fsdp", scatter_dimension=0, tiled=True
    ).astype(F32)
    feed_gain_part = jnp.sum(normed_two_grad * unit_two, axis=0)
    residual_grad = own_gradient.astype(F32) + norm_back(
        normed_two_grad * gain_two, unit_two, inverse_two
    )
    mixed_part = lax.psum_scatter(
        dot(hidden, down_weight).astype(BF16), "fsdp", scatter_dimension=0, tiled=True
    )
    mixed = move((residual + mixed_part.astype(F32)).astype(BF16), back_pairs)

    down_term = dot_tn(hidden, out_gradient).astype(BF16)
    gate_term = dot_tn(normed_two, gate_grad).astype(BF16).reshape(nf, weight_rows, hidden_cols)
    up_term = dot_tn(normed_two, up_grad).astype(BF16).reshape(nf, weight_rows, hidden_cols)
    gate_got = exchange(lambda d: pick(gate_term, d))
    up_got = exchange(lambda d: pick(up_term, d))

    branch_grad = residual_grad.astype(BF16)
    output_term = lax.psum_scatter(
        dot_tn(attended, branch_grad).astype(BF16), "fsdp", scatter_dimension=0, tiled=True
    )
    attended_grad = dot_nt(branch_grad, output_matrix).astype(BF16)
    attended_grad = attended_grad.reshape(rows, key_heads, wide).transpose(1, 0, 2)
    head_grad = assembled(exchange(lambda d: pick(attended_grad, d // share), share), share)
    group_grad = by_group(head_grad.reshape(held * rows, repeat, head))
    query_back, key_back, value_back = attend_backward(
        group_query, group_key, group_value, group_grad, log_total, group_segment, group_index, scale
    )
    query_turned = turned(from_group(query_back).astype(F32), tables, -1.0)
    query_norm_part = jnp.sum(query_turned * query_unit, axis=(0, 1))
    query_proj_grad = norm_back(query_turned * query_norm, query_unit, query_inverse).astype(BF16)
    key_turned = turned(from_group(key_back[:, None]).astype(F32), tables, -1.0)
    key_norm_part = jnp.sum(key_turned * key_unit, axis=(0, 1))
    key_proj_grad = norm_back(key_turned * key_norm, key_unit, key_inverse).astype(BF16)
    qkv_grad = jnp.concatenate(
        [
            query_proj_grad.reshape(-1, wide),
            key_proj_grad.reshape(-1, head),
            from_group(value_back[:, None]).reshape(-1, head),
        ],
        axis=1,
    )
    qkv_term = dot_tn(normed_mine, qkv_grad).astype(BF16).reshape(nf, weight_rows, -1)
    qkv_got = exchange(lambda d: pick(qkv_term, d))
    if share == 2:
        qkv_got = {
            k: (qkv_got[k].astype(F32) + qkv_got[k + 1].astype(F32)).astype(BF16)
            for k in range(0, nf, 2)
        }
    normed_one_part = dot_nt(qkv_grad, qkv_matrix).astype(BF16)
    if share == 2:
        normed_one_part = normed_one_part.reshape(held, 1, rows, width)
        empty = jnp.zeros_like(normed_one_part)
        mine_first = jnp.concatenate([normed_one_part, empty], axis=1)
        mine_last = jnp.concatenate([empty, normed_one_part], axis=1)
        normed_one_part = jnp.where(me % 2 == 0, mine_first, mine_last).reshape(nf * rows, width)
    normed_one_grad = lax.psum_scatter(
        normed_one_part, "fsdp", scatter_dimension=0, tiled=True
    ).astype(F32)
    attention_gain_part = jnp.sum(normed_one_grad * unit_one, axis=0)
    input_gradient = (
        residual_grad + norm_back(normed_one_grad * gain_one, unit_one, inverse_one)
    ).astype(BF16)
    input_gradient = move(input_gradient, back_pairs)

    down_pieces = 4
    down_chunks = list(down_term.reshape(down_pieces, -1, width))
    gate_keys, qkv_keys = list(gate_got), list(qkv_got)
    sums = line_sums(
        down_chunks
        + [gate_got[k] for k in gate_keys]
        + [up_got[k] for k in gate_keys]
        + [output_term]
        + [qkv_got[k] for k in qkv_keys]
    )
    down_total = jnp.concatenate(sums[:down_pieces], axis=0).astype(F32)
    sums = sums[down_pieces:]
    gate_total = assembled(dict(zip(gate_keys, sums))).transpose(1, 0, 2)
    sums = sums[nf:]
    up_total = assembled(dict(zip(gate_keys, sums))).transpose(1, 0, 2)
    sums = sums[nf:]
    output_total = sums[0].astype(F32)
    qkv_total = assembled(dict(zip(qkv_keys, sums[1:])), share).transpose(1, 0, 2).astype(F32)

    gains = lax.psum(
        jnp.concatenate([attention_gain_part, feed_gain_part, query_norm_part, key_norm_part]),
        ("seq", "fsdp"),
    )

    def owned(start, size):
        return lax.dynamic_slice_in_dim(gains, start + me * size, size)

    return (
        mixed[None],
        input_gradient[None],
        owned(0, weight_rows),
        qkv_total[:, :, :wide].reshape(weight_rows, -1),
        qkv_total[:, :, wide : wide + head].reshape(weight_rows, -1),
        qkv_total[:, :, wide + head :].reshape(weight_rows, -1),
        owned(2 * width, head // nf),
        owned(2 * width + head, head // nf),
        output_total,
        owned(width, weight_rows),
        gate_total.astype(F32).reshape(weight_rows, -1),
        up_total.astype(F32).reshape(weight_rows, -1),
        down_total,
    )


def solution(mesh):
    tokens, vector, matrix = P("fsdp", "seq", None), P("fsdp"), P("fsdp", None)
    placed = (tokens, vector, matrix, matrix, matrix, vector, vector, matrix)
    placed += (vector, matrix, matrix, matrix, tokens, P(), P())
    results = (tokens, tokens, vector, matrix, matrix, matrix, vector, vector, matrix)
    results += (vector, matrix, matrix, matrix)
    return jax.shard_map(body, mesh=mesh, in_specs=placed, out_specs=results, check_vma=False)
```

```python
import functools

import jax
import jax.numpy as jnp
from jax import lax
from jax.experimental import pallas as pl
from jax.experimental.pallas import tpu as pltpu
from jax.sharding import PartitionSpec as P

EPSILON = 1e-06
ROPE_BASE = 1000000.0
NEGATIVE = -1e30
F32 = jnp.float32
BF16 = jnp.bfloat16


def relocation(ns, nf):
    pairs = []
    for s in range(ns):
        for g in range(nf):
            p, c = divmod(g, 2)
            pairs.append((s * nf + g, p * nf + 2 * (p ^ s ^ (ns // 2 * c)) + c))
    return pairs


def block_of(group, quarter, plane, ns):
    return 2 * (quarter ^ plane ^ (ns // 2 * group)) + group


def move(values, pairs):
    return lax.ppermute(values, ("seq", "fsdp"), pairs)


def pick(blocks, index):
    return lax.dynamic_index_in_dim(blocks, index, 0, keepdims=False)


def after(value, *others):
    return lax.optimization_barrier((value, others))[0]


def head_swap(values, share):
    nf = lax.axis_size("fsdp")
    among = None
    if share > 1:
        among = [[d for d in range(nf) if d % share == j] for j in range(share)]
    return lax.all_to_all(values, "fsdp", 0, 0, axis_index_groups=among, tiled=True)


def spread(values):
    return lax.all_to_all(values, "fsdp", 0, 0, tiled=True)


def line_sums(chunks):
    ns = lax.axis_size("seq")
    if ns != 4:
        return [lax.psum(c, "seq") for c in chunks]
    me = lax.axis_index("seq")
    outer = (me == 0) | (me == 3)
    inward, outward = [(0, 1), (3, 2)], [(1, 0), (2, 3)]
    count = len(chunks)
    part, total, sums = {}, {}, [None] * count
    token = None
    for step in range(count + 2):
        sends = []
        new = chunks[step] if step < count else None
        old = total[step - 2] if step >= 2 else None
        if new is not None and old is not None and new.shape == old.shape:
            sends.append((jnp.where(outer, new, old), inward + outward, ("in", "out")))
        else:
            if new is not None:
                sends.append((new, inward, ("in",)))
            if old is not None:
                sends.append((old, outward, ("out",)))
        if 1 <= step <= count:
            sends.append((part[step - 1], [(1, 2), (2, 1)], ("across",)))
        operands = [send[0] for send in sends]
        if token is not None:
            operands, _ = lax.optimization_barrier((operands, token))
        token = []
        for operand, (_, pairs, roles) in zip(operands, sends):
            got = lax.ppermute(operand, "seq", pairs)
            token.append(got)
            if "in" in roles:
                part[step] = add_rounded(new, got)
            if "out" in roles:
                sums[step - 2] = (got, old)
            if "across" in roles:
                total[step - 1] = add_rounded(part[step - 1], got)
    return [jnp.where(outer, got, mine) for got, mine in sums]


def add_rounded(left, right):
    return (left.astype(F32) + right.astype(F32)).astype(BF16)


def dot(left, right):
    return jnp.dot(left, right, preferred_element_type=F32)


def dot_nt(left, right):
    return lax.dot_general(left, right, (((1,), (1,)), ((), ())), preferred_element_type=F32)


def dot_tn(left, right):
    return lax.dot_general(left, right, (((0,), (0,)), ((), ())), preferred_element_type=F32)


def norm_back(gradient, unit_rows, inverse):
    return inverse * (gradient - unit_rows * jnp.mean(gradient * unit_rows, axis=-1, keepdims=True))


def inverse_rms(values):
    return lax.rsqrt(jnp.mean(values * values, axis=-1, keepdims=True) + EPSILON)


def rope_tables(position, head):
    half = head // 2
    exponent = jnp.arange(half, dtype=F32) * (2.0 / head)
    angles = position.astype(F32)[:, None] * (ROPE_BASE ** (-exponent))[None, :]
    cosine, sine = jnp.cos(angles), jnp.sin(angles)
    return jnp.concatenate([cosine, cosine], axis=1), jnp.concatenate([-sine, sine], axis=1)


def half_turn(values):
    return pltpu.roll(values, values.shape[1] // 2, 1)


def column(values, part, head):
    return values[:, part * head : (part + 1) * head]


def allowed_keys(begin, i, j, rows):
    shape = (begin.shape[0], rows)
    key_index = j * rows + lax.broadcasted_iota(jnp.int32, shape, 1)
    row = lax.broadcasted_iota(jnp.int32, (rows, 1), 0)
    query_index = i * rows + jnp.concatenate([row] * (begin.shape[0] // rows), axis=0)
    return (key_index >= begin) & (key_index <= query_index)


def attend_kernel(
    repeat, scale, lead_ref, x_ref, w_ref, qg_ref, kg_ref, cos_ref, sin_ref, begin_ref,
    proj_ref, qkv_ref, out_ref, key_all, value_all, score_all,
):
    rows, head = cos_ref.shape
    i, ns = pl.program_id(1), pl.num_programs(1)
    low = lead_ref[2 + pl.program_id(0) * ns + i]
    proj = dot(x_ref[...], w_ref[...])
    cosine, sine = cos_ref[...], sin_ref[...]

    def turned(part, gain):
        values = column(proj, part, head)
        normed = values * inverse_rms(values) * gain
        return (normed * cosine + half_turn(normed) * sine).astype(BF16)

    queries = [turned(part, qg_ref[...]) for part in range(repeat)]
    key = turned(repeat, kg_ref[...])
    value = column(proj, repeat + 1, head).astype(BF16)
    proj_ref[...] = proj[:, : (repeat + 1) * head]
    qkv_ref[...] = jnp.concatenate(queries + [key, value], axis=1)
    own = pl.ds(pl.multiple_of(i * rows, rows), rows)
    key_all[own, :] = key
    value_all[own, :] = value
    query = jnp.concatenate(queries, axis=0)
    begin = jnp.concatenate([begin_ref[...]] * repeat, axis=0)

    def score(j, top):
        keys = key_all[pl.ds(pl.multiple_of(j * rows, rows), rows), :]
        scores = jnp.where(allowed_keys(begin, i, j, rows), dot_nt(query, keys) * scale, NEGATIVE)
        score_all[j] = scores
        return jnp.maximum(top, jnp.max(scores, axis=1, keepdims=True))

    top = lax.fori_loop(low, i + 1, score, jnp.full((repeat * rows, 1), NEGATIVE, F32))

    def gather(j, carry):
        total, result = carry
        weights = jnp.exp(score_all[j] - top)
        values = value_all[pl.ds(pl.multiple_of(j * rows, rows), rows), :]
        total = total + jnp.sum(weights, axis=1, keepdims=True)
        return total, result + dot(weights.astype(BF16), values)

    start = (jnp.zeros((repeat * rows, 1), F32), jnp.zeros((repeat * rows, head), F32))
    total, result = lax.fori_loop(low, i + 1, gather, start)
    result = (result / total).astype(BF16)
    out_ref[...] = jnp.concatenate(
        [result[part * rows : (part + 1) * rows] for part in range(repeat)], axis=1
    )


def attend_back_kernel(
    repeat, scale, share, lead_ref, grad_ref, qkv_ref, proj_ref, w_ref, qg_ref, kg_ref, cos_ref,
    sin_ref, begin_ref, dqkv_ref, part_ref, gain_ref, score_all, prob_all, key_sum, value_sum,
):
    rows, head = cos_ref.shape
    c, ns = pl.program_id(0), pl.num_programs(1)
    i = ns - 1 - pl.program_id(1)
    low = lead_ref[2 + c * ns + i]
    cosine, sine = cos_ref[...], sin_ref[...]

    @pl.when(pl.program_id(1) == 0)
    def _():
        key_sum[...] = jnp.zeros_like(key_sum)
        value_sum[...] = jnp.zeros_like(value_sum)

    @pl.when((pl.program_id(1) == 0) & (c == 0))
    def _():
        gain_ref[...] = jnp.zeros_like(gain_ref)

    def block(j, part):
        slot = block_of(c + lead_ref[1], j, lead_ref[0], ns) // share
        place = pl.ds(pl.multiple_of(slot * rows, rows), rows)
        return qkv_ref[place, part * head : (part + 1) * head]

    query = jnp.concatenate([block(i, part) for part in range(repeat)], axis=0)
    grad = jnp.concatenate([column(grad_ref, part, head) for part in range(repeat)], axis=0)
    begin = jnp.concatenate([begin_ref[...]] * repeat, axis=0)

    def score(j, top):
        scores = dot_nt(query, block(j, repeat)) * scale
        scores = jnp.where(allowed_keys(begin, i, j, rows), scores, NEGATIVE)
        score_all[j] = scores
        prob_all[j] = dot_nt(grad, block(j, repeat + 1))
        return jnp.maximum(top, jnp.max(scores, axis=1, keepdims=True))

    top = lax.fori_loop(low, i + 1, score, jnp.full((repeat * rows, 1), NEGATIVE, F32))

    def weigh(j, carry):
        total, delta = carry
        weights = jnp.exp(score_all[j] - top)
        score_all[j] = weights
        total = total + jnp.sum(weights, axis=1, keepdims=True)
        return total, delta + jnp.sum(weights * prob_all[j], axis=1, keepdims=True)

    zero = jnp.zeros((repeat * rows, 1), F32)
    total, delta = lax.fori_loop(low, i + 1, weigh, (zero, zero))
    inverse_total = 1.0 / total
    delta = delta * inverse_total

    def back(j, query_sum):
        place = pl.ds(pl.multiple_of(j * rows, rows), rows)
        probs = score_all[j] * inverse_total
        score_grad = (probs * (prob_all[j] - delta)).astype(BF16)
        key_sum[place, :] += dot_tn(score_grad, query)
        value_sum[place, :] += dot_tn(probs.astype(BF16), grad)
        return query_sum + dot(score_grad, block(j, repeat))

    query_grad = lax.fori_loop(low, i + 1, back, jnp.zeros((repeat * rows, head), F32)) * scale
    own = pl.ds(pl.multiple_of(i * rows, rows), rows)
    key_grad = key_sum[own, :] * scale

    def unturned(gradient, part, gain):
        values = column(proj_ref, part, head)
        inverse = inverse_rms(values)
        unit = values * inverse
        turned = gradient * cosine - half_turn(gradient) * sine
        gained = jnp.sum(turned * unit, axis=0, keepdims=True)
        return norm_back(turned * gain, unit, inverse).astype(BF16), gained

    pieces, query_gained = [], 0.0
    for part in range(repeat):
        piece, gained = unturned(
            query_grad[part * rows : (part + 1) * rows], part, qg_ref[...]
        )
        pieces.append(piece)
        query_gained = query_gained + gained
    piece, key_gained = unturned(key_grad, repeat, kg_ref[...])
    gain_ref[0:1, :] += query_gained
    gain_ref[1:2, :] += key_gained
    dqkv = jnp.concatenate(pieces + [piece, value_sum[own, :].astype(BF16)], axis=1)
    dqkv_ref[...] = dqkv
    part_ref[...] = dot_nt(dqkv, w_ref[...]).astype(BF16)


def attention_calls(ns, share, rows, width, repeat, head, scale):
    groups, held = 2 // share, 2 * ns // share
    columns = (repeat + 2) * head
    span = ns * rows

    def inside(flip, divide):
        def index(c, t, lead):
            quarter = ns - 1 - t if flip else t
            return block_of(c + lead[1], quarter, lead[0], ns) // divide, 0

        return index

    def whole(shape):
        return pl.BlockSpec(shape, lambda c, t, lead: (0, 0))

    def specs(flip):
        held_block = lambda size: pl.BlockSpec((rows, size), inside(flip, share))
        common = [whole((1, head)), whole((1, head)), held_block(head), held_block(head), held_block(1)]
        return held_block, common

    scores = pltpu.VMEM((ns, repeat * rows, rows), F32)
    held_block, common = specs(False)
    flops = 2 * held * rows * width * columns
    forward = pl.pallas_call(
        functools.partial(attend_kernel, repeat, scale),
        grid_spec=pltpu.PrefetchScalarGridSpec(
            num_scalar_prefetch=1,
            grid=(groups, ns),
            in_specs=[pl.BlockSpec((rows, width), inside(False, 1)), whole((width, columns))] + common,
            out_specs=[held_block((repeat + 1) * head), held_block(columns), held_block(repeat * head)],
            scratch_shapes=[pltpu.VMEM((span, head), BF16), pltpu.VMEM((span, head), BF16), scores],
        ),
        out_shape=[
            jax.ShapeDtypeStruct((held * rows, (repeat + 1) * head), F32),
            jax.ShapeDtypeStruct((held * rows, columns), BF16),
            jax.ShapeDtypeStruct((held * rows, repeat * head), BF16),
        ],
        cost_estimate=pl.CostEstimate(flops=2 * flops, bytes_accessed=20 << 20, transcendentals=4 << 20),
        name="attend",
    )
    held_block, common = specs(True)
    backward = pl.pallas_call(
        functools.partial(attend_back_kernel, repeat, scale, share),
        grid_spec=pltpu.PrefetchScalarGridSpec(
            num_scalar_prefetch=1,
            grid=(groups, ns),
            in_specs=[
                held_block(repeat * head),
                whole((held * rows, columns)),
                held_block((repeat + 1) * head),
                whole((width, columns)),
            ]
            + common,
            out_specs=[held_block(columns), held_block(width), whole((8, head))],
            scratch_shapes=[scores, scores, pltpu.VMEM((span, head), F32), pltpu.VMEM((span, head), F32)],
        ),
        out_shape=[
            jax.ShapeDtypeStruct((held * rows, columns), BF16),
            jax.ShapeDtypeStruct((held * rows, width), BF16),
            jax.ShapeDtypeStruct((8, head), F32),
        ],
        cost_estimate=pl.CostEstimate(flops=4 * flops, bytes_accessed=30 << 20, transcendentals=4 << 20),
        name="attend_back",
    )
    return forward, backward


def body(
    tokens,
    attention_gain,
    query_weight,
    key_projection_weight,
    value_projection_weight,
    query_gain,
    key_gain,
    output_weight,
    feed_gain,
    gate_weight,
    up_weight,
    down_weight,
    cotangent,
    seq_lengths,
    dealing,
):
    ns, nf = lax.axis_size("seq"), lax.axis_size("fsdp")
    plane, me = lax.axis_index("seq"), lax.axis_index("fsdp")
    rows, width = tokens.shape[1], tokens.shape[2]
    slots = dealing.shape[0] // nf
    head = query_gain.shape[0] * nf
    key_heads = key_projection_weight.shape[1] // head
    repeat = query_weight.shape[1] // head // key_heads
    share = nf // key_heads
    assert nf == 2 * ns and share in (1, 2) and key_heads * share == nf
    held = nf // share
    wide = repeat * head
    columns = wide + 2 * head
    weight_rows = query_weight.shape[0]
    hidden_cols = gate_weight.shape[1] // nf
    pairs = relocation(ns, nf)
    back_pairs = [(b, a) for a, b in pairs]
    attend, attend_back = attention_calls(ns, share, rows, width, repeat, head, head ** (-0.5))

    inputs = move(tokens[0], pairs).astype(F32)
    own_gradient = move(after(cotangent[0], inputs[:8, :128]), pairs)

    gains = jnp.concatenate([attention_gain, feed_gain, query_gain, key_gain])
    gains = jnp.pad(gains, (0, -gains.shape[0] % 128))
    gains = lax.all_gather(gains, "fsdp", axis=0, tiled=True).reshape(nf, -1).astype(F32)
    cuts = [weight_rows, 2 * weight_rows, 2 * weight_rows + head // nf, 2 * weight_rows + 2 * head // nf]
    gain_one, gain_two, query_norm, key_norm = (
        part.reshape(1, -1) for part in jnp.split(gains, cuts, axis=1)[:4]
    )

    qkv_local = jnp.concatenate(
        [
            query_weight.reshape(weight_rows, key_heads, wide),
            key_projection_weight.reshape(weight_rows, key_heads, head),
            value_projection_weight.reshape(weight_rows, key_heads, head),
        ],
        axis=2,
    ).transpose(1, 0, 2)
    qkv_matrix = spread(jnp.repeat(qkv_local, share, axis=0)).reshape(width, columns)
    output_matrix = lax.all_gather(output_weight, "fsdp", axis=0, tiled=True)

    block_ids = jnp.arange(nf, dtype=jnp.int32)
    if share == 2:
        block_ids = 2 * jnp.arange(held, dtype=jnp.int32) + me % 2
    parity = block_ids % 2
    quarter = (block_ids // 2) ^ plane ^ (ns // 2 * parity)
    row_index = quarter[:, None] * rows + jnp.arange(rows, dtype=jnp.int32)[None, :]
    dealt = lax.dynamic_slice_in_dim(dealing, plane * 2 * slots, 2 * slots)
    numbers = jnp.arange(seq_lengths.shape[0], dtype=jnp.int32)
    lengths = jnp.sum(jnp.where(dealt[:, None] == numbers[None, :], seq_lengths[None, :], 0), axis=1)
    ends = jnp.cumsum(lengths.reshape(2, slots), axis=1)

    def begins(index, group_ends):
        passed = index[:, :, None] >= group_ends[:, None, :]
        return jnp.max(jnp.where(passed, group_ends[:, None, :], 0), axis=2)

    begin = begins(row_index, jnp.where((parity == 0)[:, None], ends[0][None, :], ends[1][None, :]))
    cosine, sine = rope_tables((row_index - begin).reshape(-1), head)
    begin = begin.reshape(-1, 1)
    firsts = jnp.broadcast_to(jnp.arange(ns, dtype=jnp.int32)[None, :] * rows, (2, ns))
    lows = begins(firsts, ends) // rows
    first_group = me % 2 if share == 2 else jnp.zeros((), jnp.int32)
    if share == 2:
        lows = pick(lows, first_group)
    lead = jnp.concatenate([plane[None], first_group[None], lows.reshape(-1)]).astype(jnp.int32)

    inverse_one = inverse_rms(inputs)
    unit_one = inputs * inverse_one
    normed_one = lax.all_gather((unit_one * gain_one).astype(BF16), "fsdp", axis=0, tiled=True)

    proj, qkv, head_result = attend(
        lead, normed_one, qkv_matrix, query_norm, key_norm, cosine, sine, begin
    )
    attended = head_swap(head_result.reshape(held, rows, wide), share)
    attended = attended.transpose(1, 0, 2).reshape(rows, key_heads * wide)
    residual = inputs + dot(attended, output_matrix)

    inner_local = jnp.concatenate(
        [
            gate_weight.reshape(weight_rows, nf, hidden_cols),
            up_weight.reshape(weight_rows, nf, hidden_cols),
        ],
        axis=2,
    ).transpose(1, 0, 2)
    inner_matrix = spread(after(inner_local, normed_one[:8, :128])).reshape(width, 2 * hidden_cols)
    out_gradient = lax.all_gather(
        after(own_gradient, normed_one[:8, :128]), "fsdp", axis=0, tiled=True
    )
    hidden_grad = dot_nt(out_gradient, down_weight)

    inverse_two = inverse_rms(residual)
    unit_two = residual * inverse_two
    normed_two = lax.all_gather((unit_two * gain_two).astype(BF16), "fsdp", axis=0, tiled=True)
    inner = dot(normed_two, inner_matrix)
    gate_value, up_value = inner[:, :hidden_cols], inner[:, hidden_cols:]
    sigmoid_gate = jax.nn.sigmoid(gate_value)
    hidden = (gate_value * sigmoid_gate * up_value).astype(BF16)
    up_grad = (hidden_grad * gate_value * sigmoid_gate).astype(BF16)
    gate_grad = (
        hidden_grad * up_value * sigmoid_gate * (1.0 + gate_value * (1.0 - sigmoid_gate))
    ).astype(BF16)
    inner_grad = jnp.concatenate([gate_grad, up_grad], axis=1)
    normed_two_part = dot_nt(inner_grad, inner_matrix).astype(BF16)
    normed_two_grad = lax.psum_scatter(
        normed_two_part, "fsdp", scatter_dimension=0, tiled=True
    ).astype(F32)
    feed_gain_part = jnp.sum(normed_two_grad * unit_two, axis=0)
    residual_grad = own_gradient.astype(F32) + norm_back(
        normed_two_grad * gain_two, unit_two, inverse_two
    )

    down_term = dot_tn(after(hidden, normed_two_part[:8, :128]), out_gradient).astype(BF16)
    inner_term = dot_tn(after(normed_two, down_term[:8, :128]), inner_grad).astype(BF16)
    inner_got = spread(inner_term.reshape(nf, weight_rows, 2 * hidden_cols))
    mixed_part = dot(after(hidden, inner_term[:8, :128]), down_weight).astype(BF16)

    branch_grad = residual_grad.astype(BF16)
    attended_grad = dot_nt(branch_grad, output_matrix).astype(BF16)
    attended_grad = attended_grad.reshape(rows, key_heads, wide).transpose(1, 0, 2)
    head_grad = head_swap(attended_grad, share).reshape(held * rows, wide)
    output_term = lax.psum_scatter(
        dot_tn(attended, branch_grad).astype(BF16), "fsdp", scatter_dimension=0, tiled=True
    )
    qkv_grad, normed_one_part, norm_parts = attend_back(
        lead, head_grad, qkv, proj, qkv_matrix, query_norm, key_norm, cosine, sine, begin
    )
    normed_mine = normed_one
    if share == 2:
        normed_mine = pick(
            normed_one.reshape(held, 2, rows, width).transpose(1, 0, 2, 3), first_group
        ).reshape(held * rows, width)
        normed_one_part = normed_one_part.reshape(held, 1, rows, width)
        empty = jnp.zeros_like(normed_one_part)
        mine_first = jnp.concatenate([normed_one_part, empty], axis=1)
        mine_last = jnp.concatenate([empty, normed_one_part], axis=1)
        normed_one_part = jnp.where(me % 2 == 0, mine_first, mine_last).reshape(nf * rows, width)
    normed_one_grad = lax.psum_scatter(
        normed_one_part, "fsdp", scatter_dimension=0, tiled=True
    ).astype(F32)
    qkv_term = dot_tn(normed_mine, qkv_grad).astype(BF16)
    qkv_got = spread(qkv_term.reshape(nf, weight_rows, columns))
    if share == 2:
        qkv_got = qkv_got.astype(F32).reshape(key_heads, 2, weight_rows, columns)
        qkv_got = jnp.sum(qkv_got, axis=1).astype(BF16)
    attention_gain_part = jnp.sum(normed_one_grad * unit_one, axis=0)
    input_gradient = (
        residual_grad + norm_back(normed_one_grad * gain_one, unit_one, inverse_one)
    ).astype(BF16)
    input_gradient = move(input_gradient, back_pairs)
    mixed_part = lax.psum_scatter(
        after(mixed_part, normed_one_grad[:8, :128]), "fsdp", scatter_dimension=0, tiled=True
    )
    mixed = move((residual + mixed_part.astype(F32)).astype(BF16), back_pairs)

    down_pieces, inner_pieces, qkv_pieces = 2, 4, 2
    sums = line_sums(
        list(down_term.reshape(down_pieces, -1, width))
        + list(inner_got.reshape(inner_pieces, -1, 2 * hidden_cols))
        + [output_term]
        + list(qkv_got.reshape(qkv_pieces, -1, columns))
    )
    down_total = jnp.concatenate(sums[:down_pieces], axis=0).astype(F32)
    sums = sums[down_pieces:]
    inner_total = jnp.concatenate(sums[:inner_pieces], axis=0).reshape(nf, weight_rows, -1)
    inner_total = inner_total.transpose(1, 0, 2).astype(F32)
    sums = sums[inner_pieces:]
    output_total = sums[0].astype(F32)
    qkv_total = jnp.concatenate(sums[1:], axis=0).reshape(key_heads, weight_rows, columns)
    qkv_total = qkv_total.transpose(1, 0, 2).astype(F32)

    parts = jnp.concatenate(
        [attention_gain_part, feed_gain_part, norm_parts[0], norm_parts[1]]
    ).reshape(-1, 128)
    parts = lax.all_gather(parts, ("seq", "fsdp"), axis=0)
    gain_sums = jnp.sum(parts, axis=0).reshape(-1)

    def owned(start, size):
        return lax.dynamic_slice_in_dim(gain_sums, start + me * size, size)

    return (
        mixed[None],
        input_gradient[None],
        owned(0, weight_rows),
        qkv_total[:, :, :wide].reshape(weight_rows, -1),
        qkv_total[:, :, wide : wide + head].reshape(weight_rows, -1),
        qkv_total[:, :, wide + head :].reshape(weight_rows, -1),
        owned(2 * width, head // nf),
        owned(2 * width + head, head // nf),
        output_total,
        owned(width, weight_rows),
        inner_total[:, :, :hidden_cols].reshape(weight_rows, -1),
        inner_total[:, :, hidden_cols:].reshape(weight_rows, -1),
        down_total,
    )


def solution(mesh):
    tokens, vector, matrix = P("fsdp", "seq", None), P("fsdp"), P("fsdp", None)
    placed = (tokens, vector, matrix, matrix, matrix, vector, vector, matrix)
    placed += (vector, matrix, matrix, matrix, tokens, P(), P())
    results = (tokens, tokens, vector, matrix, matrix, matrix, vector, vector, matrix)
    results += (vector, matrix, matrix, matrix)
    return jax.shard_map(body, mesh=mesh, in_specs=placed, out_specs=results, check_vma=False)
```

```python
import functools

import jax
import jax.numpy as jnp
from jax import lax
from jax.experimental import pallas as pl
from jax.experimental.pallas import tpu as pltpu
from jax.sharding import PartitionSpec as P

EPSILON = 1e-06
ROPE_BASE = 1000000.0
NEGATIVE = -1e30
F32 = jnp.float32
BF16 = jnp.bfloat16


def plane_of(group, ns):
    return group // 2 if group % 2 == 0 else ns - 1 - group // 2


def relocation(ns, nf):
    pairs = []
    for s in range(ns):
        for g in range(nf):
            p, c = plane_of(g, ns), g % 2
            pairs.append((s * nf + g, p * nf + 2 * (p ^ s ^ (ns // 2 * c)) + c))
    return pairs


def block_of(group, quarter, plane, ns):
    return 2 * (quarter ^ plane ^ (ns // 2 * group)) + group


def move(values, pairs):
    return lax.ppermute(values, ("seq", "fsdp"), pairs)


def pick(blocks, index):
    return lax.dynamic_index_in_dim(blocks, index, 0, keepdims=False)


def after(value, *others):
    return pl.pallas_call(
        lambda *refs: None,
        out_shape=jax.ShapeDtypeStruct(value.shape, value.dtype),
        in_specs=[pl.BlockSpec(memory_space=pl.ANY)] * (1 + len(others)),
        out_specs=pl.BlockSpec(memory_space=pl.ANY),
        input_output_aliases={0: 0},
        cost_estimate=pl.CostEstimate(flops=0, bytes_accessed=0, transcendentals=0),
        name="after",
    )(value, *others)


def head_swap(values, share):
    nf = lax.axis_size("fsdp")
    among = None
    if share > 1:
        among = [[d for d in range(nf) if d % share == j] for j in range(share)]
    return lax.all_to_all(values, "fsdp", 0, 0, axis_index_groups=among, tiled=True)


def spread(values):
    return lax.all_to_all(values, "fsdp", 0, 0, tiled=True)


def gather_by_permutes(values):
    nf, me = lax.axis_size("fsdp"), lax.axis_index("fsdp")
    kept = {0: values}
    for k in range(2, nf, 2):
        kept[k] = swap(values, k)
    crossed = swap(jnp.stack([kept[k] for k in sorted(kept)]), 1)
    buffer = jnp.zeros((nf,) + values.shape, values.dtype)
    for number, k in enumerate(sorted(kept)):
        buffer = lax.dynamic_update_index_in_dim(buffer, kept[k], me ^ k, 0)
        buffer = lax.dynamic_update_index_in_dim(buffer, crossed[number], me ^ k ^ 1, 0)
    return buffer.reshape((-1,) + values.shape[1:])


def swap(values, k):
    n = lax.axis_size("fsdp")
    return lax.ppermute(values, "fsdp", [(i, i ^ k) for i in range(n)])


def share_over_seq(piece):
    ns, me = lax.axis_size("seq"), lax.axis_index("seq")
    buffer = jnp.zeros((ns,) + piece.shape, piece.dtype)
    buffer = lax.dynamic_update_index_in_dim(buffer, piece, me, 0)
    for r in range(1, ns):
        got = lax.ppermute(piece, "seq", [(i, (i + r) % ns) for i in range(ns)])
        buffer = lax.dynamic_update_index_in_dim(buffer, got, (me + ns - r) % ns, 0)
    return buffer


def line_sums(chunks, lanes=2):
    ns = lax.axis_size("seq")
    if ns != 4:
        totals = [lax.psum(c, "seq") for c in chunks]
        return [(t, t) for t in totals]
    me = lax.axis_index("seq")
    outer = (me == 0) | (me == 3)
    inward, outward = [(0, 1), (3, 2)], [(1, 0), (2, 3)]
    count = len(chunks)
    part, total, sums = {}, {}, [None] * count
    tokens = {}
    for step in range(count + 2 * lanes):
        sends = []
        new = chunks[step] if step < count else None
        old = total.get(step - 2 * lanes)
        if new is not None and old is not None and new.shape == old.shape:
            sends.append((jnp.where(outer, new, old), inward + outward, ("in", "out")))
        else:
            if new is not None:
                sends.append((new, inward, ("in",)))
            if old is not None:
                sends.append((old, outward, ("out",)))
        if step - lanes in part:
            sends.append((part[step - lanes], [(1, 2), (2, 1)], ("across",)))
        waited = tokens.get(step - lanes)
        tokens[step] = []
        for operand, pairs, roles in sends:
            if waited:
                operand = after(operand, *waited)
            got = lax.ppermute(operand, "seq", pairs)
            tokens[step].append(got)
            if "in" in roles:
                part[step] = add_rounded(new, got)
            if "out" in roles:
                sums[step - 2 * lanes] = (got, old)
            if "across" in roles:
                total[step - lanes] = add_rounded(part[step - lanes], got)
    return sums


def finish_kernel(sizes, lead_ref, got_ref, mine_ref, *refs):
    start = 0
    take = lead_ref[0] == 1
    for size, out in zip(sizes, refs[-len(sizes) :]):
        got = got_ref[0, :, start : start + size].astype(F32)
        mine = mine_ref[0, :, start : start + size].astype(F32)
        out[...] = jnp.where(take, got, mine)
        start += size


def finished(chunks, sizes, blocks):
    ns, me = lax.axis_size("seq"), lax.axis_index("seq")
    take = ((me == 0) | (me == ns - 1)).astype(jnp.int32)[None]
    first, outs = 0, None
    for got, mine in chunks:
        count, rows, width = got.shape
        taken = pl.BlockSpec((1, rows, width), lambda b, lead: (b, 0, 0))
        held = [] if outs is None else list(outs)
        outs = pl.pallas_call(
            functools.partial(finish_kernel, sizes),
            grid_spec=pltpu.PrefetchScalarGridSpec(
                num_scalar_prefetch=1,
                grid=(count,),
                in_specs=[taken, taken] + [pl.BlockSpec(memory_space=pl.ANY)] * len(held),
                out_specs=[
                    pl.BlockSpec((rows, size), lambda b, lead, first=first: (0, first + b))
                    for size in sizes
                ],
            ),
            out_shape=[jax.ShapeDtypeStruct((rows, blocks * size), F32) for size in sizes],
            input_output_aliases={3 + i: i for i in range(len(held))},
            cost_estimate=pl.CostEstimate(
                flops=0, bytes_accessed=8 * count * rows * width, transcendentals=0
            ),
            name="finish",
        )(take, got, mine, *held)
        first += count
    return outs


def add_rounded(left, right):
    return (left.astype(F32) + right.astype(F32)).astype(BF16)


def dot(left, right):
    return jnp.dot(left, right, preferred_element_type=F32)


def dot_nt(left, right):
    return lax.dot_general(left, right, (((1,), (1,)), ((), ())), preferred_element_type=F32)


def dot_tn(left, right):
    return lax.dot_general(left, right, (((0,), (0,)), ((), ())), preferred_element_type=F32)


def norm_back(gradient, unit_rows, inverse):
    return inverse * (gradient - unit_rows * jnp.mean(gradient * unit_rows, axis=-1, keepdims=True))


def inverse_rms(values):
    return lax.rsqrt(jnp.mean(values * values, axis=-1, keepdims=True) + EPSILON)


def rope_tables(position, head):
    half = head // 2
    exponent = jnp.arange(half, dtype=F32) * (2.0 / head)
    angles = position.astype(F32)[:, None] * (ROPE_BASE ** (-exponent))[None, :]
    cosine, sine = jnp.cos(angles), jnp.sin(angles)
    return jnp.concatenate([cosine, cosine], axis=1), jnp.concatenate([-sine, sine], axis=1)


def half_turn(values):
    return pltpu.roll(values, values.shape[1] // 2, 1)


def column(values, part, head):
    return values[:, part * head : (part + 1) * head]


def allowed_keys(begin, i, j, rows):
    shape = (begin.shape[0], rows)
    key_index = j * rows + lax.broadcasted_iota(jnp.int32, shape, 1)
    row = lax.broadcasted_iota(jnp.int32, (rows, 1), 0)
    query_index = i * rows + jnp.concatenate([row] * (begin.shape[0] // rows), axis=0)
    return (key_index >= begin) & (key_index <= query_index)


def attend_kernel(
    repeat, scale, lead_ref, x_ref, w_ref, qg_ref, kg_ref, cos_ref, sin_ref, begin_ref,
    proj_ref, qkv_ref, out_ref, key_all, value_all, score_all,
):
    rows, head = cos_ref.shape
    i, ns = pl.program_id(1), pl.num_programs(1)
    low = lead_ref[2 + pl.program_id(0) * ns + i]
    proj = dot(x_ref[...], w_ref[...])
    cosine, sine = cos_ref[...], sin_ref[...]

    def turned(part, gain):
        values = column(proj, part, head)
        normed = values * inverse_rms(values) * gain
        return (normed * cosine + half_turn(normed) * sine).astype(BF16)

    queries = [turned(part, qg_ref[...]) for part in range(repeat)]
    key = turned(repeat, kg_ref[...])
    value = column(proj, repeat + 1, head).astype(BF16)
    proj_ref[...] = proj[:, : (repeat + 1) * head]
    qkv_ref[...] = jnp.concatenate(queries + [key, value], axis=1)
    own = pl.ds(pl.multiple_of(i * rows, rows), rows)
    key_all[own, :] = key
    value_all[own, :] = value
    query = jnp.concatenate(queries, axis=0)
    begin = jnp.concatenate([begin_ref[...]] * repeat, axis=0)

    def score(j, top):
        keys = key_all[pl.ds(pl.multiple_of(j * rows, rows), rows), :]
        scores = jnp.where(allowed_keys(begin, i, j, rows), dot_nt(query, keys) * scale, NEGATIVE)
        score_all[j] = scores
        return jnp.maximum(top, jnp.max(scores, axis=1, keepdims=True))

    top = lax.fori_loop(low, i + 1, score, jnp.full((repeat * rows, 1), NEGATIVE, F32))

    def gather(j, carry):
        total, result = carry
        weights = jnp.exp(score_all[j] - top)
        values = value_all[pl.ds(pl.multiple_of(j * rows, rows), rows), :]
        total = total + jnp.sum(weights, axis=1, keepdims=True)
        return total, result + dot(weights.astype(BF16), values)

    start = (jnp.zeros((repeat * rows, 1), F32), jnp.zeros((repeat * rows, head), F32))
    total, result = lax.fori_loop(low, i + 1, gather, start)
    result = (result / total).astype(BF16)
    out_ref[...] = jnp.concatenate(
        [result[part * rows : (part + 1) * rows] for part in range(repeat)], axis=1
    )


def attend_back_kernel(
    repeat, scale, share, lead_ref, grad_ref, qkv_ref, proj_ref, w_ref, qg_ref, kg_ref, cos_ref,
    sin_ref, begin_ref, dqkv_ref, part_ref, gain_ref, score_all, prob_all, key_sum, value_sum,
):
    rows, head = cos_ref.shape
    c, ns = pl.program_id(0), pl.num_programs(1)
    i = ns - 1 - pl.program_id(1)
    low = lead_ref[2 + c * ns + i]
    cosine, sine = cos_ref[...], sin_ref[...]

    @pl.when(pl.program_id(1) == 0)
    def _():
        key_sum[...] = jnp.zeros_like(key_sum)
        value_sum[...] = jnp.zeros_like(value_sum)

    @pl.when((pl.program_id(1) == 0) & (c == 0))
    def _():
        gain_ref[...] = jnp.zeros_like(gain_ref)

    def block(j, part):
        slot = block_of(c + lead_ref[1], j, lead_ref[0], ns) // share
        place = pl.ds(pl.multiple_of(slot * rows, rows), rows)
        return qkv_ref[place, part * head : (part + 1) * head]

    query = jnp.concatenate([block(i, part) for part in range(repeat)], axis=0)
    grad = jnp.concatenate([column(grad_ref, part, head) for part in range(repeat)], axis=0)
    begin = jnp.concatenate([begin_ref[...]] * repeat, axis=0)

    def score(j, top):
        scores = dot_nt(query, block(j, repeat)) * scale
        scores = jnp.where(allowed_keys(begin, i, j, rows), scores, NEGATIVE)
        score_all[j] = scores
        prob_all[j] = dot_nt(grad, block(j, repeat + 1))
        return jnp.maximum(top, jnp.max(scores, axis=1, keepdims=True))

    top = lax.fori_loop(low, i + 1, score, jnp.full((repeat * rows, 1), NEGATIVE, F32))

    def weigh(j, carry):
        total, delta = carry
        weights = jnp.exp(score_all[j] - top)
        score_all[j] = weights
        total = total + jnp.sum(weights, axis=1, keepdims=True)
        return total, delta + jnp.sum(weights * prob_all[j], axis=1, keepdims=True)

    zero = jnp.zeros((repeat * rows, 1), F32)
    total, delta = lax.fori_loop(low, i + 1, weigh, (zero, zero))
    inverse_total = 1.0 / total
    delta = delta * inverse_total

    def back(j, query_sum):
        place = pl.ds(pl.multiple_of(j * rows, rows), rows)
        probs = score_all[j] * inverse_total
        score_grad = (probs * (prob_all[j] - delta)).astype(BF16)
        key_sum[place, :] += dot_tn(score_grad, query)
        value_sum[place, :] += dot_tn(probs.astype(BF16), grad)
        return query_sum + dot(score_grad, block(j, repeat))

    query_grad = lax.fori_loop(low, i + 1, back, jnp.zeros((repeat * rows, head), F32)) * scale
    own = pl.ds(pl.multiple_of(i * rows, rows), rows)
    key_grad = key_sum[own, :] * scale

    def unturned(gradient, part, gain):
        values = column(proj_ref, part, head)
        inverse = inverse_rms(values)
        unit = values * inverse
        turned = gradient * cosine - half_turn(gradient) * sine
        gained = jnp.sum(turned * unit, axis=0, keepdims=True)
        return norm_back(turned * gain, unit, inverse).astype(BF16), gained

    pieces, query_gained = [], 0.0
    for part in range(repeat):
        piece, gained = unturned(
            query_grad[part * rows : (part + 1) * rows], part, qg_ref[...]
        )
        pieces.append(piece)
        query_gained = query_gained + gained
    piece, key_gained = unturned(key_grad, repeat, kg_ref[...])
    gain_ref[0:1, :] += query_gained
    gain_ref[1:2, :] += key_gained
    dqkv = jnp.concatenate(pieces + [piece, value_sum[own, :].astype(BF16)], axis=1)
    dqkv_ref[...] = dqkv
    part_ref[...] = dot_nt(dqkv, w_ref[...]).astype(BF16)


def attention_calls(ns, share, rows, width, repeat, head, scale):
    groups, held = 2 // share, 2 * ns // share
    columns = (repeat + 2) * head
    span = ns * rows

    def inside(flip, divide):
        def index(c, t, lead):
            quarter = ns - 1 - t if flip else t
            return block_of(c + lead[1], quarter, lead[0], ns) // divide, 0

        return index

    def whole(shape):
        return pl.BlockSpec(shape, lambda c, t, lead: (0, 0))

    def specs(flip):
        held_block = lambda size: pl.BlockSpec((rows, size), inside(flip, share))
        common = [whole((1, head)), whole((1, head)), held_block(head), held_block(head), held_block(1)]
        return held_block, common

    scores = pltpu.VMEM((ns, repeat * rows, rows), F32)
    held_block, common = specs(False)
    flops = 2 * held * rows * width * columns
    forward = pl.pallas_call(
        functools.partial(attend_kernel, repeat, scale),
        grid_spec=pltpu.PrefetchScalarGridSpec(
            num_scalar_prefetch=1,
            grid=(groups, ns),
            in_specs=[pl.BlockSpec((rows, width), inside(False, 1)), whole((width, columns))] + common,
            out_specs=[held_block((repeat + 1) * head), held_block(columns), held_block(repeat * head)],
            scratch_shapes=[pltpu.VMEM((span, head), BF16), pltpu.VMEM((span, head), BF16), scores],
        ),
        out_shape=[
            jax.ShapeDtypeStruct((held * rows, (repeat + 1) * head), F32),
            jax.ShapeDtypeStruct((held * rows, columns), BF16),
            jax.ShapeDtypeStruct((held * rows, repeat * head), BF16),
        ],
        cost_estimate=pl.CostEstimate(flops=2 * flops, bytes_accessed=20 << 20, transcendentals=4 << 20),
        name="attend",
    )
    held_block, common = specs(True)
    backward = pl.pallas_call(
        functools.partial(attend_back_kernel, repeat, scale, share),
        grid_spec=pltpu.PrefetchScalarGridSpec(
            num_scalar_prefetch=1,
            grid=(groups, ns),
            in_specs=[
                held_block(repeat * head),
                whole((held * rows, columns)),
                held_block((repeat + 1) * head),
                whole((width, columns)),
            ]
            + common,
            out_specs=[held_block(columns), held_block(width), whole((8, head))],
            scratch_shapes=[scores, scores, pltpu.VMEM((span, head), F32), pltpu.VMEM((span, head), F32)],
        ),
        out_shape=[
            jax.ShapeDtypeStruct((held * rows, columns), BF16),
            jax.ShapeDtypeStruct((held * rows, width), BF16),
            jax.ShapeDtypeStruct((8, head), F32),
        ],
        cost_estimate=pl.CostEstimate(flops=4 * flops, bytes_accessed=30 << 20, transcendentals=4 << 20),
        name="attend_back",
    )
    return forward, backward


def body(
    tokens,
    attention_gain,
    query_weight,
    key_projection_weight,
    value_projection_weight,
    query_gain,
    key_gain,
    output_weight,
    feed_gain,
    gate_weight,
    up_weight,
    down_weight,
    cotangent,
    seq_lengths,
    dealing,
):
    ns, nf = lax.axis_size("seq"), lax.axis_size("fsdp")
    plane, me = lax.axis_index("seq"), lax.axis_index("fsdp")
    rows, width = tokens.shape[1], tokens.shape[2]
    slots = dealing.shape[0] // nf
    head = query_gain.shape[0] * nf
    key_heads = key_projection_weight.shape[1] // head
    repeat = query_weight.shape[1] // head // key_heads
    share = nf // key_heads
    assert nf == 2 * ns and share in (1, 2) and key_heads * share == nf
    held = nf // share
    wide = repeat * head
    columns = wide + 2 * head
    weight_rows = query_weight.shape[0]
    hidden_cols = gate_weight.shape[1] // nf
    pairs = relocation(ns, nf)
    back_pairs = [(b, a) for a, b in pairs]
    attend, attend_back = attention_calls(ns, share, rows, width, repeat, head, head ** (-0.5))

    moved = move(tokens[0], pairs)
    inputs = moved.astype(F32)
    own_gradient = move(after(cotangent[0], moved), pairs)

    gains = jnp.concatenate([attention_gain, feed_gain, query_gain, key_gain])
    gains = jnp.pad(gains, (0, -gains.shape[0] % 128))
    gains = spread(jnp.broadcast_to(gains[None, None, :], (nf, 1, gains.shape[0])))
    gains = gains.reshape(nf, -1).astype(F32)
    cuts = [weight_rows, 2 * weight_rows, 2 * weight_rows + head // nf, 2 * weight_rows + 2 * head // nf]
    gain_one, gain_two, query_norm, key_norm = (
        part.reshape(1, -1) for part in jnp.split(gains, cuts, axis=1)[:4]
    )

    qkv_local = jnp.concatenate(
        [
            query_weight.reshape(weight_rows, key_heads, wide),
            key_projection_weight.reshape(weight_rows, key_heads, head),
            value_projection_weight.reshape(weight_rows, key_heads, head),
        ],
        axis=2,
    ).transpose(1, 0, 2)
    qkv_matrix = spread(after(jnp.repeat(qkv_local, share, axis=0))).reshape(width, columns)

    part_cols = 2 * hidden_cols // ns
    inner_local = jnp.where(plane < ns // 2, gate_weight, up_weight)
    inner_local = lax.dynamic_index_in_dim(
        inner_local.reshape(weight_rows, nf, ns // 2, part_cols), plane % (ns // 2), 2, keepdims=False
    ).transpose(1, 0, 2)
    inner_part = spread(after(inner_local)).reshape(width, part_cols)
    output_matrix = lax.all_gather(output_weight, "fsdp", axis=0, tiled=True)

    block_ids = jnp.arange(nf, dtype=jnp.int32)
    if share == 2:
        block_ids = 2 * jnp.arange(held, dtype=jnp.int32) + me % 2
    parity = block_ids % 2
    quarter = (block_ids // 2) ^ plane ^ (ns // 2 * parity)
    row_index = quarter[:, None] * rows + jnp.arange(rows, dtype=jnp.int32)[None, :]
    dealt = jnp.concatenate(
        [
            lax.dynamic_slice_in_dim(dealing, plane * 2 * slots, slots),
            lax.dynamic_slice_in_dim(dealing, (ns - 1 - plane) * 2 * slots + slots, slots),
        ]
    )
    numbers = jnp.arange(seq_lengths.shape[0], dtype=jnp.int32)
    lengths = jnp.sum(jnp.where(dealt[:, None] == numbers[None, :], seq_lengths[None, :], 0), axis=1)
    ends = jnp.cumsum(lengths.reshape(2, slots), axis=1)

    def begins(index, group_ends):
        passed = index[:, :, None] >= group_ends[:, None, :]
        return jnp.max(jnp.where(passed, group_ends[:, None, :], 0), axis=2)

    begin = begins(row_index, jnp.where((parity == 0)[:, None], ends[0][None, :], ends[1][None, :]))
    cosine, sine = rope_tables((row_index - begin).reshape(-1), head)
    begin = begin.reshape(-1, 1)
    firsts = jnp.broadcast_to(jnp.arange(ns, dtype=jnp.int32)[None, :] * rows, (2, ns))
    lows = begins(firsts, ends) // rows
    first_group = me % 2 if share == 2 else jnp.zeros((), jnp.int32)
    if share == 2:
        lows = pick(lows, first_group)
    lead = jnp.concatenate([plane[None], first_group[None], lows.reshape(-1)]).astype(jnp.int32)

    inverse_one = inverse_rms(inputs)
    unit_one = inputs * inverse_one
    normed_own = after((unit_one * gain_one).astype(BF16), qkv_matrix, inner_part)
    normed_one = lax.all_gather(normed_own, "fsdp", axis=0, tiled=True)
    inner_matrix = share_over_seq(after(inner_part, own_gradient))
    inner_matrix = inner_matrix.transpose(1, 0, 2).reshape(width, 2 * hidden_cols)
    out_gradient = gather_by_permutes(after(own_gradient, normed_one))
    hidden_grad = dot_nt(out_gradient, down_weight)

    proj, qkv, head_result = attend(
        lead, normed_one, qkv_matrix, query_norm, key_norm, cosine, sine, begin
    )
    attended = head_swap(head_result.reshape(held, rows, wide), share)
    attended = attended.transpose(1, 0, 2).reshape(rows, key_heads * wide)
    residual = inputs + dot(attended, output_matrix)

    inverse_two = inverse_rms(residual)
    unit_two = residual * inverse_two
    normed_two = lax.all_gather((unit_two * gain_two).astype(BF16), "fsdp", axis=0, tiled=True)
    inner = dot(normed_two, inner_matrix)
    gate_value, up_value = inner[:, :hidden_cols], inner[:, hidden_cols:]
    sigmoid_gate = jax.nn.sigmoid(gate_value)
    hidden = (gate_value * sigmoid_gate * up_value).astype(BF16)
    up_grad = (hidden_grad * gate_value * sigmoid_gate).astype(BF16)
    gate_grad = (
        hidden_grad * up_value * sigmoid_gate * (1.0 + gate_value * (1.0 - sigmoid_gate))
    ).astype(BF16)
    inner_grad = jnp.concatenate([gate_grad, up_grad], axis=1)
    normed_two_part = dot_nt(inner_grad, inner_matrix).astype(BF16)
    down_term = dot_tn(hidden, out_gradient).astype(BF16)
    inner_term = dot_tn(normed_two, inner_grad).astype(BF16)
    normed_two_grad = lax.psum_scatter(
        normed_two_part, "fsdp", scatter_dimension=0, tiled=True
    )
    normed_two_grad = after(normed_two_grad, down_term, inner_term).astype(F32)
    inner_got = spread(inner_term.reshape(nf, weight_rows, 2 * hidden_cols))
    feed_gain_part = jnp.sum(normed_two_grad * unit_two, axis=0)
    residual_grad = own_gradient.astype(F32) + norm_back(
        normed_two_grad * gain_two, unit_two, inverse_two
    )

    branch_grad = residual_grad.astype(BF16)
    attended_grad = dot_nt(branch_grad, output_matrix).astype(BF16)
    attended_grad = attended_grad.reshape(rows, key_heads, wide).transpose(1, 0, 2)
    head_grad = head_swap(attended_grad, share).reshape(held * rows, wide)
    output_term = lax.psum_scatter(
        dot_tn(attended, branch_grad).astype(BF16), "fsdp", scatter_dimension=0, tiled=True
    )
    qkv_grad, normed_one_part, norm_parts = attend_back(
        lead, head_grad, qkv, proj, qkv_matrix, query_norm, key_norm, cosine, sine, begin
    )
    normed_mine = normed_one
    if share == 2:
        normed_mine = pick(
            normed_one.reshape(held, 2, rows, width).transpose(1, 0, 2, 3), first_group
        ).reshape(held * rows, width)
        normed_one_part = normed_one_part.reshape(held, 1, rows, width)
        empty = jnp.zeros_like(normed_one_part)
        mine_first = jnp.concatenate([normed_one_part, empty], axis=1)
        mine_last = jnp.concatenate([empty, normed_one_part], axis=1)
        normed_one_part = jnp.where(me % 2 == 0, mine_first, mine_last).reshape(nf * rows, width)
    normed_one_grad = lax.psum_scatter(
        normed_one_part, "fsdp", scatter_dimension=0, tiled=True
    ).astype(F32)
    qkv_term = dot_tn(normed_mine, qkv_grad).astype(BF16)
    qkv_got = spread(qkv_term.reshape(nf, weight_rows, columns))
    if share == 2:
        qkv_got = qkv_got.astype(F32).reshape(key_heads, 2, weight_rows, columns)
        qkv_got = jnp.sum(qkv_got, axis=1).astype(BF16)
    attention_gain_part = jnp.sum(normed_one_grad * unit_one, axis=0)
    input_gradient = (
        residual_grad + norm_back(normed_one_grad * gain_one, unit_one, inverse_one)
    ).astype(BF16)
    input_gradient = move(input_gradient, back_pairs)
    mixed_part = dot(after(hidden, normed_one_part), down_weight).astype(BF16)
    mixed_part = lax.psum_scatter(mixed_part, "fsdp", scatter_dimension=0, tiled=True)
    mixed = move((residual + mixed_part.astype(F32)).astype(BF16), back_pairs)

    down_pieces, inner_pieces, qkv_pieces = 4, nf, 4
    sums = line_sums(
        list(down_term.reshape(down_pieces, -1, width))
        + list(inner_got.reshape(inner_pieces, -1, weight_rows, 2 * hidden_cols))
        + [output_term]
        + list(qkv_got.reshape(qkv_pieces, -1, weight_rows, columns))
    )
    outer = (plane == 0) | (plane == ns - 1)

    def settled(pairs_of):
        return jnp.concatenate([jnp.where(outer, g, m) for g, m in pairs_of], axis=0).astype(F32)

    down_total = settled(sums[:down_pieces])
    sums = sums[down_pieces:]
    gate_total, up_total = finished(sums[:inner_pieces], [hidden_cols, hidden_cols], nf)
    sums = sums[inner_pieces:]
    output_total = settled(sums[:1])
    query_total, key_total, value_total = finished(sums[1:], [wide, head, head], key_heads)

    parts = jnp.concatenate(
        [
            part.reshape(nf, -1)
            for part in (attention_gain_part, feed_gain_part, norm_parts[0], norm_parts[1])
        ],
        axis=1,
    )
    parts = jnp.pad(parts, ((0, 0), (0, -parts.shape[1] % 128)))
    parts = jnp.broadcast_to(parts[None], (ns,) + parts.shape).reshape(ns * nf, 1, -1)
    parts = lax.all_to_all(parts, ("seq", "fsdp"), 0, 0, tiled=True)
    gain_sums = jnp.sum(parts, axis=(0, 1))
    sizes = [weight_rows, weight_rows, head // nf, head // nf]
    ends_at = [sum(sizes[: i + 1]) for i in range(4)]
    attention_gain_total, feed_gain_total, query_gain_total, key_gain_total = (
        gain_sums[end - size : end] for end, size in zip(ends_at, sizes)
    )

    return (
        mixed[None],
        input_gradient[None],
        attention_gain_total,
        query_total,
        key_total,
        value_total,
        query_gain_total,
        key_gain_total,
        output_total,
        feed_gain_total,
        gate_total,
        up_total,
        down_total,
    )


def solution(mesh):
    tokens, vector, matrix = P("fsdp", "seq", None), P("fsdp"), P("fsdp", None)
    placed = (tokens, vector, matrix, matrix, matrix, vector, vector, matrix)
    placed += (vector, matrix, matrix, matrix, tokens, P(), P())
    results = (tokens, tokens, vector, matrix, matrix, matrix, vector, vector, matrix)
    results += (vector, matrix, matrix, matrix)
    return jax.shard_map(body, mesh=mesh, in_specs=placed, out_specs=results, check_vma=False)
```
